32 devices in a mesh: pair: 4 (over y, core), rows: 8 (over z, x).
Axes of the slice: x: 2, y: 2, z: 4, core: 2. Of those that a mesh axis runs over, the one named last changes fastest.
Arguments:
- snapshot: float32 [1536, 2048], P('rows', 'pair'), may hold values from -40 to 40
- keep_side: int32 [2, 4], P(None, 'pair'), may hold values 0 or 1
Outputs:
- rotated: float32 [1536, 2048], P('rows', 'pair')
The draws below stay inside these ranges and needn't reach their ends.
All inputs are finite; a program needn't handle non-finite values. No bound on the sum of `keep_side` on one device may be relied on, other than what follows from the above.
Results may differ from the reference program's by a relative error of at most 0.00013.
Values sent between devices are 32-bit elements; how exact they have to be, the bound alone decides.
A program may use at most 64 MiB of HBM per device.

```python
import jax
import jax.numpy as jnp
from jax import lax

BLK = 256
ROUNDS = 2
ROWS = 1536
COLS = 2048
N_PAIR = 4


def draw_snapshot(key, part):
    keys = jax.random.split(jax.random.fold_in(key, 7), 1)
    values = jax.random.normal(keys[0], (ROWS, COLS), jnp.float32)
    return jnp.clip(values, -6.0, 6.0).astype(jnp.float32)


def place_ends(result, rng, smallest, high):
    spot = [jax.random.randint(jax.random.fold_in(rng, axis), (), 0, length) for axis, length in enumerate(result.shape)]
    longest = result.shape.index(max(result.shape))
    beside = spot[:longest] + [(spot[longest] + 1) % result.shape[longest]] + spot[longest + 1:]
    return result.at[tuple(spot)].set(smallest).at[tuple(beside)].set(high)


def setup_inputs(seed: int = 0) -> dict:
    arg_keys = jax.random.split(jax.random.key(seed), 3)
    snapshot = draw_snapshot(jax.random.fold_in(arg_keys[2], 71), 0)
    keep_side = place_ends((jax.random.randint(arg_keys[1], (ROUNDS, N_PAIR), 0, 2) < 1).astype(jnp.int32), jax.random.fold_in(arg_keys[1], 1), 0, 1)
    return {"snapshot": snapshot, "keep_side": keep_side}


EPS = 1e-06

def polar_map(gram, total_rows):
    high = lax.Precision.HIGHEST
    width = gram.shape[0]
    diag_vals = jnp.diagonal(gram)
    inv_norm = lax.rsqrt(diag_vals / total_rows + EPS)
    corr = gram * inv_norm[:, None] * inv_norm[None, :] / total_rows
    scale = jnp.sqrt(jnp.sum(corr * corr) / width)
    e_mat = corr / scale
    eye = jnp.eye(width, dtype=jnp.float32)
    e_two = jnp.dot(e_mat, e_mat, precision=high)
    b_one = (9.0 * e_mat - 6.0 * e_two + jnp.dot(e_mat, e_two, precision=high)) * 0.25
    t_zero = (3.0 * eye - e_mat) * 0.5
    t_one = (3.0 * eye - b_one) * 0.5
    z_two = jnp.dot(t_zero, t_one, precision=high)
    b_two = jnp.dot(jnp.dot(b_one, t_one, precision=high), t_one, precision=high)
    t_two = (3.0 * eye - b_two) * 0.5
    z_three = jnp.dot(z_two, t_two, precision=high)
    return z_three * (inv_norm / jnp.sqrt(scale))[:, None]

def reference(snapshot, keep_side):
    high = lax.Precision.HIGHEST
    total_rows = snapshot.shape[0]
    pairs = snapshot.reshape(total_rows, N_PAIR, 2 * BLK).transpose(1, 0, 2)

    def one_pair(block):
        gram = jnp.dot(block.T, block, precision=high)
        return jnp.dot(block, polar_map(gram, total_rows), precision=high)
    for turn in range(ROUNDS):
        pairs = lax.map(one_pair, pairs)
        first = pairs[:, :, :BLK]
        second = pairs[:, :, BLK:]
        side = keep_side[turn][:, None, None]
        forward = jnp.where(side == 0, first, second)
        backward = jnp.where(side == 0, second, first)
        pairs = jnp.concatenate([jnp.roll(forward, 1, axis=0), jnp.roll(backward, -1, axis=0)], axis=2)
    return pairs.transpose(1, 0, 2).reshape(total_rows, N_PAIR * 2 * BLK)
```

```python
import functools

import jax
import jax.numpy as jnp
from jax import lax
from jax.experimental import pallas as pl
from jax.experimental.pallas import tpu as pltpu
from jax.sharding import PartitionSpec as P

ROUNDS = 2
EPS = 1e-06
TILE = 128
MESH = pl.DeviceIdType.MESH
F32 = jnp.float32
BF16 = jnp.bfloat16


def split(value):
    high = value.astype(BF16)
    low = (value - high.astype(F32)).astype(BF16)
    return high, low


def dot(a, b):
    return jnp.dot(a, b, preferred_element_type=F32)


def dot_split(a, b):
    rows = a[0].shape[0]
    both = dot(jnp.concatenate([a[0], a[1]], axis=0), b[0])
    return both[:rows] + both[rows:] + dot(a[0], b[1])


def tiles_of(width):
    count = width // TILE
    return [(i, j) for i in range(count) for j in range(i, count)]


def local_gram(left, right, acc):
    high, low = split(jnp.concatenate([left, right], axis=1))
    lhs = jnp.concatenate([high, high, low], axis=0).T
    rhs = jnp.concatenate([high, low, high], axis=0)
    width = rhs.shape[1]
    place = 0
    for i in range(width // TILE):
        strip = dot(lhs[i * TILE:(i + 1) * TILE], rhs[:, i * TILE:])
        for j in range(width // TILE - i):
            acc[place * TILE:(place + 1) * TILE, :] = strip[:, j * TILE:(j + 1) * TILE]
            place += 1


def all_reduce(n_rows, masks, acc, full, rbuf, send_sem, recv_sem):
    me = lax.axis_index("rows")
    parts = len(masks)
    steps = len(masks[0])
    length = acc.shape[0] // parts
    copies = []

    def bit(mask):
        return lax.rem(me // mask, 2)

    def peer(mask):
        return me + mask * (1 - 2 * bit(mask))

    def remote(src, dst, slot, mask):
        copy = pltpu.make_async_remote_copy(
            src_ref=src, dst_ref=dst, send_sem=send_sem.at[slot], recv_sem=recv_sem.at[slot],
            device_id={"rows": peer(mask)}, device_id_type=MESH)
        copy.start()
        copies.append(copy)
        return copy

    keep = [[part * length] for part in range(parts)]
    pending = [None] * parts
    for k in range(steps + 1):
        half = length >> (k + 1)
        for part in range(parts):
            base = part * length
            here = keep[part][-1]
            if k > 0:
                pending[part].wait_recv()
                got = rbuf[pl.ds(base + length - 2 * (length >> k), length >> k), :]
                span = pl.ds(pl.multiple_of(here, 8), length >> k)
                if k == steps:
                    full[span, :] = acc[span, :] + got
                else:
                    acc[span, :] = acc[span, :] + got
            if k < steps:
                mask = masks[part][k]
                own = bit(mask)
                keep[part].append(here + own * half)
                away = pl.multiple_of(here + (1 - own) * half, 8)
                pending[part] = remote(
                    acc.at[pl.ds(away, half), :],
                    rbuf.at[pl.ds(base + length - 2 * half, half), :],
                    part * 2 * steps + k, mask)
    for k in reversed(range(steps)):
        half = length >> (k + 1)
        for part in range(parts):
            if k < steps - 1:
                pending[part].wait_recv()
            span = pl.ds(pl.multiple_of(keep[part][k + 1], 8), half)
            pending[part] = remote(
                full.at[span, :], full.at[span, :], part * 2 * steps + steps + k, masks[part][k])
    for part in range(parts):
        pending[part].wait_recv()
    return copies


def rotate(left, right, full, total_rows):
    block = jnp.concatenate([left, right], axis=1)
    width = block.shape[1]
    count = width // TILE
    at = {pair: full[n * TILE:(n + 1) * TILE, :] for n, pair in enumerate(tiles_of(width))}
    unit = (lax.broadcasted_iota(jnp.int32, (TILE, TILE), 0)
            == lax.broadcasted_iota(jnp.int32, (TILE, TILE), 1))
    diag = [jnp.where(unit, at[i, i], 0.0) for i in range(count)]
    as_row = [lax.rsqrt(jnp.sum(d, axis=0, keepdims=True) / total_rows + EPS) for d in diag]
    as_col = [lax.rsqrt(jnp.sum(d, axis=1, keepdims=True) / total_rows + EPS) for d in diag]
    energy = jnp.zeros((1, TILE), F32)
    for i, j in tiles_of(width):
        at[i, j] = at[i, j] * as_col[i] * as_row[j] / total_rows
        part = jnp.sum(at[i, j] * at[i, j], axis=0, keepdims=True)
        energy = energy + (part if i == j else 2.0 * part)
    scale = jnp.sqrt(jnp.sum(energy, axis=1, keepdims=True) / width)
    inv_scale = 1.0 / scale
    for i, j in tiles_of(width):
        at[i, j] = at[i, j] * inv_scale
        if i != j:
            at[j, i] = at[i, j].T
    e_mat = jnp.concatenate(
        [jnp.concatenate([at[i, j] for j in range(count)], axis=1) for i in range(count)], axis=0)
    e_half = split(e_mat)
    e_two = dot_split(e_half, e_half)
    e_three = dot_split(e_half, split(e_two))
    wide = (lax.broadcasted_iota(jnp.int32, (width, width), 0)
            == lax.broadcasted_iota(jnp.int32, (width, width), 1))
    b_one = (9.0 * e_mat - 6.0 * e_two + e_three) * 0.25
    t_half = split(jnp.where(wide, 1.5, 0.0) - 0.5 * b_one)
    inv_norm = jnp.concatenate(as_row, axis=1) * lax.rsqrt(scale)
    y = block * inv_norm
    y = 1.5 * y - 0.5 * dot_split(split(y), e_half)
    y = dot_split(split(y), t_half)
    b = 3.0 * y - 2.0 * dot_split(split(y), t_half)
    b = dot_split(split(b), t_half)
    b = dot_split(split(b), t_half)
    return 1.5 * y - 0.5 * b


def kernel(n_rows, n_pair, masks, side, x, out, acc, full, rbuf, leave, land,
           row_send, row_recv, pair_send, pair_recv):
    p = lax.axis_index("pair")
    r = lax.axis_index("rows")
    after = lax.rem(p + 1, n_pair)
    before = lax.rem(p + n_pair - 1, n_pair)
    barrier = pltpu.get_barrier_semaphore()
    for mask in sorted(masks[0]):
        other = r + mask * (1 - 2 * lax.rem(r // mask, 2))
        pl.semaphore_signal(barrier, inc=1, device_id={"rows": other}, device_id_type=MESH)
    for other in (after, before):
        pl.semaphore_signal(barrier, inc=1, device_id={"pair": other}, device_id_type=MESH)
    half = x.shape[1] // 2
    local_gram(x[:, :half], x[:, half:], acc.at[0])
    pl.semaphore_wait(barrier, len(masks[0]) + 2)
    waits = []
    for turn in range(ROUNDS):
        if turn == 0:
            halves = lambda: (x[:, :half], x[:, half:])
        else:
            halves = lambda: (land[turn - 1, 0], land[turn - 1, 1])
            local_gram(*halves(), acc.at[turn])
        waits += all_reduce(n_rows, masks, acc.at[turn], full.at[turn], rbuf.at[turn],
                            row_send.at[turn], row_recv.at[turn])
        y = rotate(*halves(), full.at[turn], x.shape[0] * n_rows)
        first, second = y[:, :half], y[:, half:]
        chosen = jnp.full(first.shape, side[turn, 0], jnp.int32) == 0
        leave[turn, 0] = jnp.where(chosen, first, second)
        leave[turn, 1] = jnp.where(chosen, second, first)
        sent = []
        for way, other in enumerate((after, before)):
            copy = pltpu.make_async_remote_copy(
                src_ref=leave.at[turn, way], dst_ref=land.at[turn, way],
                send_sem=pair_send.at[turn, way], recv_sem=pair_recv.at[turn, way],
                device_id={"pair": other}, device_id_type=MESH)
            copy.start()
            sent.append(copy)
        for copy in sent:
            copy.wait_recv()
        waits += sent
    out[:, :half] = land[ROUNDS - 1, 0]
    out[:, half:] = land[ROUNDS - 1, 1]
    for copy in waits:
        copy.wait_send()


def solution(mesh):
    n_rows = mesh.shape["rows"]
    n_pair = mesh.shape["pair"]
    powers = []
    while (1 << len(powers)) < n_rows:
        powers.append(1 << len(powers))
    masks = (tuple(powers), tuple(powers[1:] + powers[:1]))
    steps = len(powers)

    def local(snapshot, keep_side):
        rows, width = snapshot.shape
        gram_rows = len(tiles_of(width)) * TILE
        vmem = pl.BlockSpec(memory_space=pltpu.VMEM)
        return pl.pallas_call(
            functools.partial(kernel, n_rows, n_pair, masks),
            out_shape=jax.ShapeDtypeStruct((rows, width), F32),
            in_specs=[pl.BlockSpec(memory_space=pltpu.SMEM), vmem],
            out_specs=vmem,
            scratch_shapes=[
                pltpu.VMEM((ROUNDS, gram_rows, TILE), F32),
                pltpu.VMEM((ROUNDS, gram_rows, TILE), F32),
                pltpu.VMEM((ROUNDS, gram_rows, TILE), F32),
                pltpu.VMEM((ROUNDS, 2, rows, width // 2), F32),
                pltpu.VMEM((ROUNDS, 2, rows, width // 2), F32),
                pltpu.SemaphoreType.DMA((ROUNDS, 4 * steps)),
                pltpu.SemaphoreType.DMA((ROUNDS, 4 * steps)),
                pltpu.SemaphoreType.DMA((ROUNDS, 2)),
                pltpu.SemaphoreType.DMA((ROUNDS, 2)),
            ],
            compiler_params=pltpu.CompilerParams(
                collective_id=0, has_side_effects=True, vmem_limit_bytes=48 << 20),
        )(keep_side, snapshot)

    placed = (P("rows", "pair"), P(None, "pair"))
    return jax.shard_map(
        local, mesh=mesh, in_specs=placed, out_specs=P("rows", "pair"), check_vma=False
    )
```

```python
import functools

import jax
import jax.numpy as jnp
from jax import lax
from jax.experimental import pallas as pl
from jax.experimental.pallas import tpu as pltpu
from jax.sharding import PartitionSpec as P

ROUNDS = 2
EPS = 1e-06
TILE = 128
PARTS = 4
FAR = (0, 2)
MESH = pl.DeviceIdType.MESH
F32 = jnp.float32
BF16 = jnp.bfloat16


def split(value):
    high = value.astype(BF16)
    low = (value - high.astype(F32)).astype(BF16)
    return high, low


def dot(a, b):
    return jnp.dot(a, b, preferred_element_type=F32)


def dot_split(a, b):
    rows = a[0].shape[0]
    both = dot(jnp.concatenate([a[0], a[1]], axis=0), b[0])
    return both[:rows] + both[rows:] + dot(a[0], b[1])


def off_diagonal(count):
    return [(i, j) for i in range(count) for j in range(i + 1, count)]


def packed_rows(width, unit):
    count = width // TILE
    body = (count * (count - 1) // 2 + count // 2) * TILE
    return -(-(body + 8 * (count // 2)) // unit) * unit


def square_index():
    return (lax.broadcasted_iota(jnp.int32, (TILE, TILE), 0),
            lax.broadcasted_iota(jnp.int32, (TILE, TILE), 1))


def gram_pieces(left, right, acc):
    high, low = split(jnp.concatenate([left, right], axis=1))
    lhs = jnp.concatenate([high, high, low], axis=0).T
    rhs = jnp.concatenate([high, low, high], axis=0)
    count = rhs.shape[1] // TILE
    row, col = square_index()
    strips = {}

    def tile(i, j):
        if i not in strips:
            strips[i] = dot(lhs[i * TILE:(i + 1) * TILE], rhs[:, i * TILE:])
        return strips[i][:, (j - i) * TILE:(j - i + 1) * TILE]

    place = 0
    for i, j in off_diagonal(count):
        yield place, tile(i, j)
        place += TILE
    tails = []
    for i in range(0, count, 2):
        later = tile(i + 1, i + 1)
        tails.append(jnp.sum(jnp.where(row == col, later, 0.0), axis=0, keepdims=True))
        yield place, jnp.where(row <= col, tile(i, i), later)
        place += TILE
    for tail in tails:
        yield place, jnp.broadcast_to(tail, (8, TILE))
        place += 8
    if place < acc.shape[0]:
        yield place, jnp.zeros((acc.shape[0] - place, TILE), F32)


def unpacked(full, count):
    row, col = square_index()
    at, place = {}, 0
    for pair in off_diagonal(count):
        at[pair] = full[place:place + TILE, :]
        place += TILE
    tail = place + count // 2 * TILE
    for i in range(0, count, 2):
        both = full[place:place + TILE, :]
        flipped = both.T
        diagonal = jnp.broadcast_to(full[tail:tail + 1, :], (TILE, TILE))
        at[i, i] = jnp.where(row <= col, both, flipped)
        at[i + 1, i + 1] = jnp.where(row > col, both, jnp.where(row == col, diagonal, flipped))
        place += TILE
        tail += 8
    return at


def all_reduce(plan, pieces, acc, full, rbuf, send_sem, recv_sem):
    me = lax.axis_index("rows")
    parts = len(plan)
    steps = len(plan[0][2])
    copies = []

    def bit(mask):
        return lax.rem(me // mask, 2)

    def remote(src, dst, slot, mask):
        copy = pltpu.make_async_remote_copy(
            src_ref=src, dst_ref=dst, send_sem=send_sem.at[slot], recv_sem=recv_sem.at[slot],
            device_id={"rows": me + mask * (1 - 2 * bit(mask))}, device_id_type=MESH)
        copy.start()
        copies.append(copy)
        return copy

    keep = [[start] for start, _, _ in plan]
    pending = [None] * parts
    slots = 2 * steps - 1
    filled = 0
    for k in range(steps + 1):
        for part, (base, length, masks) in enumerate(plan):
            if k == 0:
                while filled < base + length:
                    place, value = next(pieces)
                    acc[place:place + value.shape[0], :] = value
                    filled = place + value.shape[0]
            size = length >> min(k, steps - 1)
            here = keep[part][-1]
            span = pl.ds(pl.multiple_of(here, 8), size)
            if k > 0:
                pending[part].wait_recv()
                landed = base + (length - 2 * size if k < steps else length - size)
                total = acc[span, :] + rbuf[pl.ds(landed, size), :]
                if k == steps:
                    full[span, :] = total
                else:
                    acc[span, :] = total
            if k < steps - 1:
                half = size // 2
                own = bit(masks[k])
                keep[part].append(here + own * half)
                away = pl.multiple_of(here + (1 - own) * half, 8)
                pending[part] = remote(
                    acc.at[pl.ds(away, half), :], rbuf.at[pl.ds(base + length - size, half), :],
                    part * slots + k, masks[k])
            elif k == steps - 1:
                pending[part] = remote(
                    acc.at[span, :], rbuf.at[pl.ds(base + length - size, size), :],
                    part * slots + k, masks[k])
    for k in reversed(range(steps - 1)):
        for part, (base, length, masks) in enumerate(plan):
            if k < steps - 2:
                pending[part].wait_recv()
            span = pl.ds(pl.multiple_of(keep[part][k + 1], 8), length >> (k + 1))
            pending[part] = remote(full.at[span, :], full.at[span, :], part * slots + steps + k, masks[k])
    if steps > 1:
        for copy in pending:
            copy.wait_recv()
    return copies


def rotate(left, right, full, total_rows):
    block = jnp.concatenate([left, right], axis=1)
    width = block.shape[1]
    count = width // TILE
    at = unpacked(full, count)
    row, col = square_index()
    unit = row == col
    diag = [jnp.where(unit, at[i, i], 0.0) for i in range(count)]
    as_row = [lax.rsqrt(jnp.sum(d, axis=0, keepdims=True) / total_rows + EPS) for d in diag]
    as_col = [lax.rsqrt(jnp.sum(d, axis=1, keepdims=True) / total_rows + EPS) for d in diag]
    energy = jnp.zeros((1, TILE), F32)
    for i, j in sorted(at):
        at[i, j] = at[i, j] * as_col[i] * as_row[j] / total_rows
        part = jnp.sum(at[i, j] * at[i, j], axis=0, keepdims=True)
        energy = energy + (part if i == j else 2.0 * part)
    scale = jnp.sqrt(jnp.sum(energy, axis=1, keepdims=True) / width)
    inv_scale = 1.0 / scale
    for i, j in sorted(at):
        at[i, j] = at[i, j] * inv_scale
        if i != j:
            at[j, i] = at[i, j].T
    e_mat = jnp.concatenate(
        [jnp.concatenate([at[i, j] for j in range(count)], axis=1) for i in range(count)], axis=0)
    e_half = split(e_mat)
    e_two = dot_split(e_half, e_half)
    e_three = dot_split(e_half, split(e_two))
    wide = (lax.broadcasted_iota(jnp.int32, (width, width), 0)
            == lax.broadcasted_iota(jnp.int32, (width, width), 1))
    b_one = (9.0 * e_mat - 6.0 * e_two + e_three) * 0.25
    t_half = split(jnp.where(wide, 1.5, 0.0) - 0.5 * b_one)
    inv_norm = jnp.concatenate(as_row, axis=1) * lax.rsqrt(scale)
    y = block * inv_norm
    y = 1.5 * y - 0.5 * dot_split(split(y), e_half)
    y = dot_split(split(y), t_half)
    b = 3.0 * y - 2.0 * dot_split(split(y), t_half)
    b = dot_split(split(b), t_half)
    b = dot_split(split(b), t_half)
    return 1.5 * y - 0.5 * b


def kernel(n_rows, n_pair, plan, side, x, out, acc, full, rbuf, leave, land,
           row_send, row_recv, pair_send, pair_recv):
    p = lax.axis_index("pair")
    r = lax.axis_index("rows")
    after = lax.rem(p + 1, n_pair)
    before = lax.rem(p + n_pair - 1, n_pair)
    barrier = pltpu.get_barrier_semaphore()
    for mask in sorted(plan[0][2]):
        other = r + mask * (1 - 2 * lax.rem(r // mask, 2))
        pl.semaphore_signal(barrier, inc=1, device_id={"rows": other}, device_id_type=MESH)
    for other in (after, before):
        pl.semaphore_signal(barrier, inc=1, device_id={"pair": other}, device_id_type=MESH)
    half = x.shape[1] // 2
    pl.semaphore_wait(barrier, len(plan[0][2]) + 2)
    waits = []
    for turn in range(ROUNDS):
        if turn == 0:
            halves = lambda: (x[:, :half], x[:, half:])
        else:
            halves = lambda: (land[turn - 1, 0], land[turn - 1, 1])
        waits += all_reduce(plan, gram_pieces(*halves(), acc.at[turn]), acc.at[turn], full.at[turn], rbuf.at[turn],
                            row_send.at[turn], row_recv.at[turn])
        y = rotate(*halves(), full.at[turn], x.shape[0] * n_rows)
        first, second = y[:, :half], y[:, half:]
        chosen = jnp.full(first.shape, side[turn, 0], jnp.int32) == 0
        leave[turn, 0] = jnp.where(chosen, first, second)
        leave[turn, 1] = jnp.where(chosen, second, first)
        sent = []
        for way, other in enumerate((after, before)):
            copy = pltpu.make_async_remote_copy(
                src_ref=leave.at[turn, way], dst_ref=land.at[turn, way],
                send_sem=pair_send.at[turn, way], recv_sem=pair_recv.at[turn, way],
                device_id={"pair": other}, device_id_type=MESH)
            copy.start()
            sent.append(copy)
        for copy in sent:
            copy.wait_recv()
        waits += sent
    out[:, :half] = land[ROUNDS - 1, 0]
    out[:, half:] = land[ROUNDS - 1, 1]
    for copy in waits:
        copy.wait_send()


def make_plan(length, unit, powers):
    near_first = tuple(powers)
    far_first = tuple(powers[1:2] + powers[:1] + powers[2:])
    units = length // unit
    plan, start = [], 0
    for part in range(PARTS):
        size = (units * (part + 1) // PARTS - units * part // PARTS) * unit
        plan.append((start, size, far_first if part in FAR else near_first))
        start += size
    return tuple(plan)


def solution(mesh):
    n_rows = mesh.shape["rows"]
    n_pair = mesh.shape["pair"]
    powers = []
    while (1 << len(powers)) < n_rows:
        powers.append(1 << len(powers))
    steps = len(powers)

    def local(snapshot, keep_side):
        rows, width = snapshot.shape
        gram_rows = packed_rows(width, 4 * n_rows)
        plan = make_plan(gram_rows, 4 * n_rows, powers)
        vmem = pl.BlockSpec(memory_space=pltpu.VMEM)
        return pl.pallas_call(
            functools.partial(kernel, n_rows, n_pair, plan),
            out_shape=jax.ShapeDtypeStruct((rows, width), F32),
            in_specs=[pl.BlockSpec(memory_space=pltpu.SMEM), vmem],
            out_specs=vmem,
            scratch_shapes=[
                pltpu.VMEM((ROUNDS, gram_rows, TILE), F32),
                pltpu.VMEM((ROUNDS, gram_rows, TILE), F32),
                pltpu.VMEM((ROUNDS, gram_rows, TILE), F32),
                pltpu.VMEM((ROUNDS, 2, rows, width // 2), F32),
                pltpu.VMEM((ROUNDS, 2, rows, width // 2), F32),
                pltpu.SemaphoreType.DMA((ROUNDS, PARTS * (2 * steps - 1))),
                pltpu.SemaphoreType.DMA((ROUNDS, PARTS * (2 * steps - 1))),
                pltpu.SemaphoreType.DMA((ROUNDS, 2)),
                pltpu.SemaphoreType.DMA((ROUNDS, 2)),
            ],
            compiler_params=pltpu.CompilerParams(
                collective_id=0, has_side_effects=True, vmem_limit_bytes=48 << 20),
        )(keep_side, snapshot)

    placed = (P("rows", "pair"), P(None, "pair"))
    return jax.shard_map(
        local, mesh=mesh, in_specs=placed, out_specs=P("rows", "pair"), check_vma=False
    )
```

```python
import functools

import jax
import jax.numpy as jnp
from jax import lax
from jax.experimental import pallas as pl
from jax.experimental.pallas import tpu as pltpu
from jax.sharding import PartitionSpec as P

ROUNDS = 2
EPS = 1e-06
TILE = 128
PARTS = 4
FAR = (1, 3)
MESH = pl.DeviceIdType.MESH
F32 = jnp.float32
BF16 = jnp.bfloat16


def split(value):
    high = value.astype(BF16)
    low = (value - high.astype(F32)).astype(BF16)
    return high, low


def dot(a, b):
    return jnp.dot(a, b, preferred_element_type=F32)


def dot_split(a, b):
    rows = a[0].shape[0]
    both = dot(jnp.concatenate([a[0], a[1]], axis=0), b[0])
    return both[:rows] + both[rows:] + dot(a[0], b[1])


def layout(count):
    mid = count // 2

    def inner(low, high):
        return ([(i, j) for i in range(low, high) for j in range(i + 1, high)]
                + [(i, i) for i in range(low, high, 2)])

    return inner(0, mid) + [(i, j) for i in range(mid) for j in range(mid, count)] + inner(mid, count)


def packed_rows(width, unit):
    count = width // TILE
    body = (count * (count - 1) // 2 + count // 2) * TILE
    return -(-(body + 8 * (count // 2)) // unit) * unit


def square_index():
    return (lax.broadcasted_iota(jnp.int32, (TILE, TILE), 0),
            lax.broadcasted_iota(jnp.int32, (TILE, TILE), 1))


def gram_pieces(near, far, count, length):
    mid = count // 2
    row, col = square_index()
    sides, strips = {}, {}

    def side(which):
        if which not in sides:
            high, low = split((far if which else near)())
            sides[which] = (jnp.concatenate([high, high, low], axis=0).T,
                            jnp.concatenate([high, low, high], axis=0))
        return sides[which]

    def tile(i, j):
        here, there = i // mid, j // mid
        first = i % mid if here == there else 0
        if (i, there) not in strips:
            lhs = side(here)[0][i % mid * TILE:(i % mid + 1) * TILE]
            strips[i, there] = dot(lhs, side(there)[1][:, first * TILE:])
        at = (j % mid - first) * TILE
        return strips[i, there][:, at:at + TILE]

    place = 0
    tails = []
    for i, j in layout(count):
        if i != j:
            value = tile(i, j)
        else:
            later = tile(i + 1, i + 1)
            tails.append(jnp.sum(jnp.where(row == col, later, 0.0), axis=0, keepdims=True))
            value = jnp.where(row <= col, tile(i, i), later)
        yield place, value
        place += TILE
    for tail in tails:
        yield place, jnp.broadcast_to(tail, (8, TILE))
        place += 8
    if place < length:
        yield place, jnp.zeros((length - place, TILE), F32)


def unpacked(full, count):
    row, col = square_index()
    at, place = {}, 0
    tail = len(layout(count)) * TILE
    for i, j in layout(count):
        both = full[place:place + TILE, :]
        place += TILE
        if i != j:
            at[i, j] = both
        else:
            flipped = both.T
            diagonal = jnp.broadcast_to(full[tail:tail + 1, :], (TILE, TILE))
            at[i, i] = jnp.where(row <= col, both, flipped)
            at[i + 1, i + 1] = jnp.where(row > col, both, jnp.where(row == col, diagonal, flipped))
            tail += 8
    return at


def all_reduce(plan, pieces, acc, full, rbuf, send_sem, recv_sem):
    me = lax.axis_index("rows")
    parts = len(plan)
    steps = len(plan[0][2])
    copies = []

    def bit(mask):
        return lax.rem(me // mask, 2)

    def remote(src, dst, slot, mask):
        copy = pltpu.make_async_remote_copy(
            src_ref=src, dst_ref=dst, send_sem=send_sem.at[slot], recv_sem=recv_sem.at[slot],
            device_id={"rows": me + mask * (1 - 2 * bit(mask))}, device_id_type=MESH)
        copy.start()
        copies.append(copy)
        return copy

    keep = [[start] for start, _, _ in plan]
    pending = [None] * parts
    slots = 2 * steps - 1
    filled = 0
    for k in range(steps + 1):
        for part, (base, length, masks) in enumerate(plan):
            if k == 0:
                while filled < base + length:
                    place, value = next(pieces)
                    acc[place:place + value.shape[0], :] = value
                    filled = place + value.shape[0]
            size = length >> min(k, steps - 1)
            here = keep[part][-1]
            span = pl.ds(pl.multiple_of(here, 8), size)
            if k > 0:
                pending[part].wait_recv()
                landed = base + (length - 2 * size if k < steps else length - size)
                total = acc[span, :] + rbuf[pl.ds(landed, size), :]
                if k == steps:
                    full[span, :] = total
                else:
                    acc[span, :] = total
            if k < steps - 1:
                half = size // 2
                own = bit(masks[k])
                keep[part].append(here + own * half)
                away = pl.multiple_of(here + (1 - own) * half, 8)
                pending[part] = remote(
                    acc.at[pl.ds(away, half), :], rbuf.at[pl.ds(base + length - size, half), :],
                    part * slots + k, masks[k])
            elif k == steps - 1:
                pending[part] = remote(
                    acc.at[span, :], rbuf.at[pl.ds(base + length - size, size), :],
                    part * slots + k, masks[k])
    for k in reversed(range(steps - 1)):
        for part, (base, length, masks) in enumerate(plan):
            if k < steps - 2:
                pending[part].wait_recv()
            span = pl.ds(pl.multiple_of(keep[part][k + 1], 8), length >> (k + 1))
            pending[part] = remote(full.at[span, :], full.at[span, :], part * slots + steps + k, masks[k])
    if steps > 1:
        for copy in pending:
            copy.wait_recv()
    return copies


def rotate(left, right, full, total_rows):
    block = jnp.concatenate([left, right], axis=1)
    width = block.shape[1]
    count = width // TILE
    at = unpacked(full, count)
    row, col = square_index()
    unit = row == col
    diag = [jnp.where(unit, at[i, i], 0.0) for i in range(count)]
    as_row = [lax.rsqrt(jnp.sum(d, axis=0, keepdims=True) / total_rows + EPS) for d in diag]
    as_col = [lax.rsqrt(jnp.sum(d, axis=1, keepdims=True) / total_rows + EPS) for d in diag]
    energy = jnp.zeros((1, TILE), F32)
    for i, j in sorted(at):
        at[i, j] = at[i, j] * as_col[i] * as_row[j] / total_rows
        part = jnp.sum(at[i, j] * at[i, j], axis=0, keepdims=True)
        energy = energy + (part if i == j else 2.0 * part)
    scale = jnp.sqrt(jnp.sum(energy, axis=1, keepdims=True) / width)
    inv_scale = 1.0 / scale
    for i, j in sorted(at):
        at[i, j] = at[i, j] * inv_scale
        if i != j:
            at[j, i] = at[i, j].T
    e_mat = jnp.concatenate(
        [jnp.concatenate([at[i, j] for j in range(count)], axis=1) for i in range(count)], axis=0)
    e_half = split(e_mat)
    e_two = dot_split(e_half, e_half)
    e_three = dot_split(e_half, split(e_two))
    wide = (lax.broadcasted_iota(jnp.int32, (width, width), 0)
            == lax.broadcasted_iota(jnp.int32, (width, width), 1))
    b_one = (9.0 * e_mat - 6.0 * e_two + e_three) * 0.25
    t_half = split(jnp.where(wide, 1.5, 0.0) - 0.5 * b_one)
    inv_norm = jnp.concatenate(as_row, axis=1) * lax.rsqrt(scale)
    y = block * inv_norm
    y = 1.5 * y - 0.5 * dot_split(split(y), e_half)
    y = dot_split(split(y), t_half)
    b = 3.0 * y - 2.0 * dot_split(split(y), t_half)
    b = dot_split(split(b), t_half)
    b = dot_split(split(b), t_half)
    return 1.5 * y - 0.5 * b


def kernel(n_rows, n_pair, plan, side, held, out, acc, full, rbuf, leave, land,
           row_send, row_recv, pair_send, pair_recv):
    p = lax.axis_index("pair")
    r = lax.axis_index("rows")
    after = lax.rem(p + 1, n_pair)
    before = lax.rem(p + n_pair - 1, n_pair)
    barrier = pltpu.get_barrier_semaphore()
    for mask in sorted(plan[0][2]):
        other = r + mask * (1 - 2 * lax.rem(r // mask, 2))
        pl.semaphore_signal(barrier, inc=1, device_id={"rows": other}, device_id_type=MESH)
    for other in (after, before):
        pl.semaphore_signal(barrier, inc=1, device_id={"pair": other}, device_id_type=MESH)
    rows, width = held.shape
    half = width // 2
    count = width // TILE
    near = 1 - lax.rem(p, 2)
    pl.semaphore_wait(barrier, len(plan[0][2]) + 2)
    waits = []
    arrived = None
    for turn in range(ROUNDS):
        def block(which, turn=turn, arrived=arrived):
            if turn == 0:
                return held[:, which * half:(which + 1) * half]
            if which not in seen:
                seen.append(which)
                arrived(which).wait_recv()
            return land[turn - 1, near + which * (1 - 2 * near)]

        seen = []
        pieces = gram_pieces(lambda: block(0), lambda: block(1), count, acc.shape[1])
        waits += all_reduce(plan, pieces, acc.at[turn], full.at[turn], rbuf.at[turn],
                            row_send.at[turn], row_recv.at[turn])
        y = rotate(block(0), block(1), full.at[turn], rows * n_rows)
        one, two = y[:, :half], y[:, half:]
        flip = near if turn else 0
        chosen = jnp.broadcast_to(side[0:1, turn:turn + 1], one.shape)
        forward = jnp.where(chosen == 0, 0, 1) == flip
        leave[turn, 0] = jnp.where(forward, one, two)
        leave[turn, 1] = jnp.where(forward, two, one)

        def remote(way, other, turn=turn):
            return pltpu.make_async_remote_copy(
                src_ref=leave.at[turn, way], dst_ref=land.at[turn, way],
                send_sem=pair_send.at[turn, way], recv_sem=pair_recv.at[turn, way],
                device_id={"pair": other}, device_id_type=MESH)

        sent = [remote(way, other) for way, other in enumerate((after, before))]
        for copy in sent:
            copy.start()
        waits += sent

        def arrived(which, remote=remote):
            return remote(near + which * (1 - 2 * near), after)

    for way, copy in enumerate(sent):
        copy.wait_recv()
        out[:, way * half:(way + 1) * half] = land[ROUNDS - 1, way]
    for copy in waits:
        copy.wait_send()


def make_plan(length, unit, powers):
    near_first = tuple(powers)
    far_first = tuple(powers[1:2] + powers[:1] + powers[2:])
    units = length // unit
    plan, start = [], 0
    for part in range(PARTS):
        size = (units * (part + 1) // PARTS - units * part // PARTS) * unit
        plan.append((start, size, far_first if part in FAR else near_first))
        start += size
    return tuple(plan)


def solution(mesh):
    n_rows = mesh.shape["rows"]
    n_pair = mesh.shape["pair"]
    powers = []
    while (1 << len(powers)) < n_rows:
        powers.append(1 << len(powers))
    steps = len(powers)

    def local(snapshot, keep_side):
        rows, width = snapshot.shape
        gram_rows = packed_rows(width, 4 * n_rows)
        plan = make_plan(gram_rows, 4 * n_rows, powers)
        vmem = pl.BlockSpec(memory_space=pltpu.VMEM)
        return pl.pallas_call(
            functools.partial(kernel, n_rows, n_pair, plan),
            out_shape=jax.ShapeDtypeStruct((rows, width), F32),
            in_specs=[vmem, vmem],
            out_specs=vmem,
            scratch_shapes=[
                pltpu.VMEM((ROUNDS, gram_rows, TILE), F32),
                pltpu.VMEM((ROUNDS, gram_rows, TILE), F32),
                pltpu.VMEM((ROUNDS, gram_rows, TILE), F32),
                pltpu.VMEM((ROUNDS, 2, rows, width // 2), F32),
                pltpu.VMEM((ROUNDS, 2, rows, width // 2), F32),
                pltpu.SemaphoreType.DMA((ROUNDS, PARTS * (2 * steps - 1))),
                pltpu.SemaphoreType.DMA((ROUNDS, PARTS * (2 * steps - 1))),
                pltpu.SemaphoreType.DMA((ROUNDS, 2)),
                pltpu.SemaphoreType.DMA((ROUNDS, 2)),
            ],
            compiler_params=pltpu.CompilerParams(
                collective_id=0, has_side_effects=True, vmem_limit_bytes=48 << 20),
        )(keep_side.T, snapshot)

    placed = (P("rows", "pair"), P(None, "pair"))
    return jax.shard_map(
        local, mesh=mesh, in_specs=placed, out_specs=P("rows", "pair"), check_vma=False
    )
```

```python
import functools

import jax
import jax.numpy as jnp
from jax import lax
from jax.experimental import pallas as pl
from jax.experimental.pallas import tpu as pltpu
from jax.sharding import PartitionSpec as P

ROUNDS = 2
EPS = 1e-06
TILE = 128
PARTS = 4
FAR = (1, 3)
MESH = pl.DeviceIdType.MESH
F32 = jnp.float32
BF16 = jnp.bfloat16


def split(value):
    high = value.astype(BF16)
    low = (value - high.astype(F32)).astype(BF16)
    return high, low


def dot(a, b):
    return jnp.dot(a, b, preferred_element_type=F32)


def dot_split(a, b):
    rows = a[0].shape[0]
    both = dot(jnp.concatenate([a[0], a[1]], axis=0), b[0])
    return both[:rows] + both[rows:] + dot(a[0], b[1])


def dot_symmetric(a, b):
    mid = a[0].shape[0] // 2
    top = dot_split((a[0][:mid], a[1][:mid]), b)
    low = dot_split((a[0][mid:], a[1][mid:]), (b[0][:, mid:], b[1][:, mid:]))
    return jnp.concatenate([top, jnp.concatenate([top[:, mid:].T, low], axis=1)], axis=0)


def layout(count):
    mid = count // 2

    def inner(low, high):
        return ([(i, j) for i in range(low, high) for j in range(i + 1, high)]
                + [(i, i) for i in range(low, high, 2)])

    return inner(0, mid) + [(i, j) for i in range(mid) for j in range(mid, count)] + inner(mid, count)


def packed_rows(width, unit):
    count = width // TILE
    body = (count * (count - 1) // 2 + count // 2) * TILE
    return -(-(body + 8 * (count // 2)) // unit) * unit


def square_index():
    return (lax.broadcasted_iota(jnp.int32, (TILE, TILE), 0),
            lax.broadcasted_iota(jnp.int32, (TILE, TILE), 1))


def gram_pieces(near, far, count, length):
    mid = count // 2
    row, col = square_index()
    sides, strips = {}, {}

    def side(which):
        if which not in sides:
            high, low = split((far if which else near)())
            sides[which] = (jnp.concatenate([high, high, low], axis=0).T,
                            jnp.concatenate([high, low, high], axis=0))
        return sides[which]

    def tile(i, j):
        here, there = i // mid, j // mid
        first = i % mid if here == there else 0
        if (i, there) not in strips:
            lhs = side(here)[0][i % mid * TILE:(i % mid + 1) * TILE]
            strips[i, there] = dot(lhs, side(there)[1][:, first * TILE:])
        at = (j % mid - first) * TILE
        return strips[i, there][:, at:at + TILE]

    place = 0
    tails = []
    for i, j in layout(count):
        if i != j:
            value = tile(i, j)
        else:
            later = tile(i + 1, i + 1)
            tails.append(jnp.sum(jnp.where(row == col, later, 0.0), axis=0, keepdims=True))
            value = jnp.where(row <= col, tile(i, i), later)
        yield place, value
        place += TILE
    for tail in tails:
        yield place, jnp.broadcast_to(tail, (8, TILE))
        place += 8
    if place < length:
        yield place, jnp.zeros((length - place, TILE), F32)


def unpacked(full, count):
    row, col = square_index()
    at, place = {}, 0
    tail = len(layout(count)) * TILE
    for i, j in layout(count):
        both = full[place:place + TILE, :]
        place += TILE
        if i != j:
            at[i, j] = both
        else:
            flipped = both.T
            diagonal = jnp.broadcast_to(full[tail:tail + 1, :], (TILE, TILE))
            at[i, i] = jnp.where(row <= col, both, flipped)
            at[i + 1, i + 1] = jnp.where(row > col, both, jnp.where(row == col, diagonal, flipped))
            tail += 8
    return at


def all_reduce(plan, pieces, acc, full, rbuf, send_sem, recv_sem):
    me = lax.axis_index("rows")
    parts = len(plan)
    steps = len(plan[0][2])
    copies = []

    def bit(mask):
        return lax.rem(me // mask, 2)

    def remote(src, dst, slot, mask):
        copy = pltpu.make_async_remote_copy(
            src_ref=src, dst_ref=dst, send_sem=send_sem.at[slot], recv_sem=recv_sem.at[slot],
            device_id={"rows": me + mask * (1 - 2 * bit(mask))}, device_id_type=MESH)
        copy.start()
        copies.append(copy)
        return copy

    keep = [[start] for start, _, _ in plan]
    pending = [None] * parts
    slots = 2 * steps - 1
    filled = 0
    for k in range(steps + 1):
        for part, (base, length, masks) in enumerate(plan):
            if k == 0:
                while filled < base + length:
                    place, value = next(pieces)
                    acc[place:place + value.shape[0], :] = value
                    filled = place + value.shape[0]
            size = length >> min(k, steps - 1)
            here = keep[part][-1]
            span = pl.ds(pl.multiple_of(here, 8), size)
            if k > 0:
                pending[part].wait_recv()
                landed = base + (length - 2 * size if k < steps else length - size)
                total = acc[span, :] + rbuf[pl.ds(landed, size), :]
                if k == steps:
                    full[span, :] = total
                else:
                    acc[span, :] = total
            if k < steps - 1:
                half = size // 2
                own = bit(masks[k])
                keep[part].append(here + own * half)
                away = pl.multiple_of(here + (1 - own) * half, 8)
                pending[part] = remote(
                    acc.at[pl.ds(away, half), :], rbuf.at[pl.ds(base + length - size, half), :],
                    part * slots + k, masks[k])
            elif k == steps - 1:
                pending[part] = remote(
                    acc.at[span, :], rbuf.at[pl.ds(base + length - size, size), :],
                    part * slots + k, masks[k])
    for k in reversed(range(steps - 1)):
        for part, (base, length, masks) in enumerate(plan):
            if k < steps - 2:
                pending[part].wait_recv()
            span = pl.ds(pl.multiple_of(keep[part][k + 1], 8), length >> (k + 1))
            pending[part] = remote(full.at[span, :], full.at[span, :], part * slots + steps + k, masks[k])
    if steps > 1:
        for copy in pending:
            copy.wait_recv()
    return copies


def rotate(left, right, full, total_rows):
    block = jnp.concatenate([left, right], axis=1)
    width = block.shape[1]
    count = width // TILE
    at = unpacked(full, count)
    row, col = square_index()
    unit = row == col
    diag = [jnp.where(unit, at[i, i], 0.0) for i in range(count)]
    as_row = [lax.rsqrt(jnp.sum(d, axis=0, keepdims=True) / total_rows + EPS) for d in diag]
    as_col = [lax.rsqrt(jnp.sum(d, axis=1, keepdims=True) / total_rows + EPS) for d in diag]
    energy = jnp.zeros((1, TILE), F32)
    for i, j in sorted(at):
        at[i, j] = at[i, j] * as_col[i] * as_row[j] / total_rows
        part = jnp.sum(at[i, j] * at[i, j], axis=0, keepdims=True)
        energy = energy + (part if i == j else 2.0 * part)
    scale = jnp.sqrt(jnp.sum(energy, axis=1, keepdims=True) / width)
    inv_scale = 1.0 / scale
    for i, j in sorted(at):
        at[i, j] = at[i, j] * inv_scale
        if i != j:
            at[j, i] = at[i, j].T
    e_mat = jnp.concatenate(
        [jnp.concatenate([at[i, j] for j in range(count)], axis=1) for i in range(count)], axis=0)
    e_half = split(e_mat)
    e_two = dot_symmetric(e_half, e_half)
    e_three = dot_symmetric(e_half, split(e_two))
    wide = (lax.broadcasted_iota(jnp.int32, (width, width), 0)
            == lax.broadcasted_iota(jnp.int32, (width, width), 1))
    b_one = (9.0 * e_mat - 6.0 * e_two + e_three) * 0.25
    t_half = split(jnp.where(wide, 1.5, 0.0) - 0.5 * b_one)
    inv_norm = jnp.concatenate(as_row, axis=1) * lax.rsqrt(scale)
    y = block * inv_norm
    y = 1.5 * y - 0.5 * dot_split(split(y), e_half)
    y = dot_split(split(y), t_half)
    b = 3.0 * y - 2.0 * dot_split(split(y), t_half)
    b = dot_split(split(b), t_half)
    b = dot_split(split(b), t_half)
    return 1.5 * y - 0.5 * b


def kernel(n_rows, n_pair, plan, side, held, out, acc, full, rbuf, leave, land,
           row_send, row_recv, pair_send, pair_recv):
    p = lax.axis_index("pair")
    r = lax.axis_index("rows")
    after = lax.rem(p + 1, n_pair)
    before = lax.rem(p + n_pair - 1, n_pair)
    barrier = pltpu.get_barrier_semaphore()
    for mask in sorted(plan[0][2]):
        other = r + mask * (1 - 2 * lax.rem(r // mask, 2))
        pl.semaphore_signal(barrier, inc=1, device_id={"rows": other}, device_id_type=MESH)
    for other in (after, before):
        pl.semaphore_signal(barrier, inc=1, device_id={"pair": other}, device_id_type=MESH)
    rows, width = held.shape
    half = width // 2
    count = width // TILE
    near = 1 - lax.rem(p, 2)
    pl.semaphore_wait(barrier, len(plan[0][2]) + 2)
    waits = []
    arrived = None
    for turn in range(ROUNDS):
        def block(which, turn=turn, arrived=arrived):
            if turn == 0:
                return held[:, which * half:(which + 1) * half]
            if which not in seen:
                seen.append(which)
                arrived(which).wait_recv()
            return land[turn - 1, near + which * (1 - 2 * near)]

        seen = []
        pieces = gram_pieces(lambda: block(0), lambda: block(1), count, acc.shape[1])
        waits += all_reduce(plan, pieces, acc.at[turn], full.at[turn], rbuf.at[turn],
                            row_send.at[turn], row_recv.at[turn])
        y = rotate(block(0), block(1), full.at[turn], rows * n_rows)
        one, two = y[:, :half], y[:, half:]
        flip = near if turn else 0
        chosen = jnp.broadcast_to(side[0:1, turn:turn + 1], one.shape)
        forward = jnp.where(chosen == 0, 0, 1) == flip
        leave[turn, 0] = jnp.where(forward, one, two)
        leave[turn, 1] = jnp.where(forward, two, one)

        def remote(way, other, turn=turn):
            return pltpu.make_async_remote_copy(
                src_ref=leave.at[turn, way], dst_ref=land.at[turn, way],
                send_sem=pair_send.at[turn, way], recv_sem=pair_recv.at[turn, way],
                device_id={"pair": other}, device_id_type=MESH)

        sent = [remote(way, other) for way, other in enumerate((after, before))]
        for copy in sent:
            copy.start()
        waits += sent

        def arrived(which, remote=remote):
            return remote(near + which * (1 - 2 * near), after)

    for way, copy in enumerate(sent):
        copy.wait_recv()
        out[:, way * half:(way + 1) * half] = land[ROUNDS - 1, way]
    for copy in waits:
        copy.wait_send()


def make_plan(length, unit, powers):
    near_first = tuple(powers)
    far_first = tuple(powers[1:2] + powers[:1] + powers[2:])
    units = length // unit
    plan, start = [], 0
    for part in range(PARTS):
        size = (units * (part + 1) // PARTS - units * part // PARTS) * unit
        plan.append((start, size, far_first if part in FAR else near_first))
        start += size
    return tuple(plan)


def solution(mesh):
    n_rows = mesh.shape["rows"]
    n_pair = mesh.shape["pair"]
    powers = []
    while (1 << len(powers)) < n_rows:
        powers.append(1 << len(powers))
    steps = len(powers)

    def local(snapshot, keep_side):
        rows, width = snapshot.shape
        gram_rows = packed_rows(width, 4 * n_rows)
        plan = make_plan(gram_rows, 4 * n_rows, powers)
        vmem = pl.BlockSpec(memory_space=pltpu.VMEM)
        return pl.pallas_call(
            functools.partial(kernel, n_rows, n_pair, plan),
            out_shape=jax.ShapeDtypeStruct((rows, width), F32),
            in_specs=[vmem, vmem],
            out_specs=vmem,
            scratch_shapes=[
                pltpu.VMEM((ROUNDS, gram_rows, TILE), F32),
                pltpu.VMEM((ROUNDS, gram_rows, TILE), F32),
                pltpu.VMEM((ROUNDS, gram_rows, TILE), F32),
                pltpu.VMEM((ROUNDS, 2, rows, width // 2), F32),
                pltpu.VMEM((ROUNDS, 2, rows, width // 2), F32),
                pltpu.SemaphoreType.DMA((ROUNDS, PARTS * (2 * steps - 1))),
                pltpu.SemaphoreType.DMA((ROUNDS, PARTS * (2 * steps - 1))),
                pltpu.SemaphoreType.DMA((ROUNDS, 2)),
                pltpu.SemaphoreType.DMA((ROUNDS, 2)),
            ],
            compiler_params=pltpu.CompilerParams(
                collective_id=0, has_side_effects=True, vmem_limit_bytes=48 << 20),
        )(keep_side.T, snapshot)

    placed = (P("rows", "pair"), P(None, "pair"))
    return jax.shard_map(
        local, mesh=mesh, in_specs=placed, out_specs=P("rows", "pair"), check_vma=False
    )
```
